256 devices in a mesh: gx: 32 (over z, x), gy: 8 (over y, core).
Axes of the slice: x: 4, y: 4, z: 8, core: 2. Of those that a mesh axis runs over, the one named last changes fastest.
Arguments:
- mode_fields: float32 [32, 2048, 2048], P(None, 'gx', 'gy'), may hold values from -60 to 60, as said below
- conductance: float32 [2048, 2048], P('gx', 'gy'), may hold values from 0.5 to 2
- potential: float32 [2048, 2048], P('gx', 'gy'), may hold values from 0.25 to 4
Outputs:
- basis_field: float32 [128, 2048, 2048], P(None, 'gx', 'gy')
- scaled_factor: float32 [128, 128], replicated
The draws below stay inside these ranges and needn't reach their ends.
Inputs may be any that keep to these rules, and one draw needn't show every extreme that they name: `mode_fields`: Real-valued mode amplitudes.
All inputs are finite; a program needn't handle non-finite values.
Results may differ from the reference program's by a relative error of at most 0.0003.
Values sent between devices are 32-bit elements; how exact they have to be, the bound alone decides.
No kernel may reach another device: no remote copies, remote signals or barrier semaphores. Data moves between devices by JAX's collectives and lax.ppermute only.
A program may use at most 64 MiB of HBM per device.

```python
import math
import jax
import jax.numpy as jnp
from jax import lax

K = 32
C = 128
CX = 64
NX = 2048
NY = 2048


def draw_mode_fields(key, part):
    key_scale, key_noise = jax.random.split(key, 2)
    col_scale = 10.0 ** jax.random.uniform(key_scale, (K, 1, 1), jnp.float32, -0.5, 0.5)
    row_pos = jnp.arange(NX, dtype=jnp.float32) / max(NX - 1, 1)
    row_scale = (10.0 ** (row_pos - 0.5))[None, :, None]
    noise = jax.random.truncated_normal(key_noise, -6.0, 6.0, (K, NX, NY), jnp.float32)
    return (col_scale * row_scale * noise).astype(jnp.float32)


def levels(own_key, dims, cuts, smallest, largest):
    def one(axis_at, shards_of):
        draws = jax.random.uniform(jax.random.fold_in(jax.random.fold_in(own_key, 6), axis_at), (shards_of,), jnp.float32, smallest / len(cuts), largest / len(cuts))
        return jnp.repeat(jnp.exp(draws), dims[axis_at] // shards_of).reshape((-1,) + (1,) * (len(dims) - axis_at - 1))

    loudness = one(*cuts[0])
    for cut in cuts[1:]:
        loudness = loudness * one(*cut)
    return loudness


def setup_inputs(seed: int = 0) -> dict:
    key_list = jax.random.split(jax.random.key(seed), 4)
    mode_fields = draw_mode_fields(jax.random.fold_in(key_list[3], 71), 0)
    conductance = jnp.clip(jnp.exp(math.log(2.0) - 1.3862944 * jax.random.uniform(key_list[1], (NX, NY), jnp.float32) ** levels(key_list[1], (NX, NY), ((0, 32), (1, 8)), -0.2, 0.2)), 0.5, 2.0)
    potential = jnp.clip(jnp.exp(math.log(4.0) - 2.7725887 * jax.random.uniform(key_list[2], (NX, NY), jnp.float32) ** levels(key_list[2], (NX, NY), ((0, 32), (1, 8)), -0.2, 0.2)), 0.25, 4.0)
    return {"mode_fields": mode_fields, "conductance": conductance, "potential": potential}


def build_columns(fields, conduct, potential):
    center = fields[:, 1:-1, 1:-1]
    k_mid = conduct[1:-1, 1:-1]
    x_plus = 0.5 * (k_mid + conduct[2:, 1:-1])
    x_minus = 0.5 * (k_mid + conduct[:-2, 1:-1])
    y_plus = 0.5 * (k_mid + conduct[1:-1, 2:])
    y_minus = 0.5 * (k_mid + conduct[1:-1, :-2])
    along_x = x_plus * (center - fields[:, 2:, 1:-1]) + x_minus * (center - fields[:, :-2, 1:-1])
    along_y = y_plus * (center - fields[:, 1:-1, 2:]) + y_minus * (center - fields[:, 1:-1, :-2])
    react = potential * center
    stacked = jnp.concatenate([center, along_x, along_y, react], 0)
    return stacked.reshape(stacked.shape[0], -1)

def reference(mode_fields, conductance, potential):
    pad_u = jnp.pad(mode_fields, ((0, 0), (1, 1), (1, 1)))
    pad_k = jnp.pad(conductance, 1)
    strips = NX // CX
    cell_count = float(NX * NY)

    def strip_columns(index):
        start = (index * CX).astype(jnp.int32)
        fields = lax.dynamic_slice_in_dim(pad_u, start, CX + 2, 1)
        conduct = lax.dynamic_slice_in_dim(pad_k, start, CX + 2, 0)
        react = lax.dynamic_slice_in_dim(potential, start, CX, 0)
        return build_columns(fields, conduct, react)

    def add_gram(carry, index):
        matrix = strip_columns(index)
        return (carry + jnp.dot(matrix, matrix.T, precision=lax.Precision.HIGHEST), None)
    indices = jnp.arange(strips, dtype=jnp.int32)
    gram_total, _ = lax.scan(add_gram, jnp.zeros((C, C), jnp.float32), indices)
    lower_tri = jnp.linalg.cholesky(gram_total / cell_count)

    def solve_strip(index):
        solved = jax.scipy.linalg.solve_triangular(lower_tri, strip_columns(index), lower=True)
        return solved.reshape(C, CX, NY)
    blocks = lax.map(solve_strip, indices)
    basis_field = blocks.transpose(1, 0, 2, 3).reshape(C, NX, NY)
    return (basis_field, lower_tri.T)
```

```python
import jax
import jax.numpy as jnp
from jax import lax
from jax.experimental import pallas as pl
from jax.experimental.pallas import tpu as pltpu
from jax.sharding import PartitionSpec as P

F32 = jnp.float32
BF16 = jnp.bfloat16
K = 32
C = 128
NB = 8


def iota(shape, dim):
    return lax.broadcasted_iota(jnp.int32, shape, dim)


def edges_kernel(rows, cols, ua_ref, ub_ref, k_ref, top_ref, bottom_ref, left_ref, right_ref):
    for ref, at in ((top_ref, 0), (bottom_ref, rows - 1)):
        ref[:K, :128] = ua_ref[pl.ds(at, K, stride=rows), :]
        ref[:K, cols - 128 :] = ub_ref[pl.ds(at, K, stride=rows), :]
        ref[K:, :] = jnp.broadcast_to(k_ref[at : at + 1, :], (8, cols))
    lane = iota((8, 128), 1)
    left = [jnp.zeros((8, 128), F32)] * (K // 8 + 1)
    right = [jnp.zeros((8, 128), F32)] * (K // 8 + 1)
    for i in range(rows):
        here = lane == i
        field_a = ua_ref[pl.ds(i, K, stride=rows), :]
        field_b = ub_ref[pl.ds(i, K, stride=rows), :]
        conduct = jnp.broadcast_to(k_ref[i : i + 1, :], (8, cols))
        for b in range(K // 8 + 1):
            if b == K // 8:
                first, last = conduct[:, :128], conduct[:, cols - 128 :]
            else:
                first, last = field_a[8 * b : 8 * b + 8], field_b[8 * b : 8 * b + 8]
            left[b] = jnp.where(here, pltpu.roll(first, i, 1) if i else first, left[b])
            right[b] = jnp.where(here, pltpu.roll(last, (i + 1) % 128, 1), right[b])
    for b in range(K // 8 + 1):
        left_ref[8 * b : 8 * b + 8, :] = left[b]
        right_ref[8 * b : 8 * b + 8, :] = right[b]


def edges(u2, conduct):
    rows, cols = conduct.shape
    whole = lambda shape: pl.BlockSpec(shape, lambda s: (0, 0))
    side = lambda t: pl.BlockSpec((K * rows, 128), lambda s: (0, t))
    sizes = [(K + 8, cols)] * 2 + [(K + 8, 128)] * 2
    return pl.pallas_call(
        lambda *refs: edges_kernel(rows, cols, *refs),
        name="edges",
        grid=(1,),
        out_shape=[jax.ShapeDtypeStruct(n, F32) for n in sizes],
        in_specs=[side(0), side(cols // 128 - 1), whole((rows, cols))],
        out_specs=[whole(n) for n in sizes],
        compiler_params=pltpu.CompilerParams(vmem_limit_bytes=16 << 20),
    )(u2, u2, conduct)


def gram_kernel(rows, cols, scale, ua_ref, ub_ref, k_ref, v_ref, up_ref, dn_ref, lf_ref, rt_ref, gram_ref, mhl_ref, acc_ref):
    step = pl.program_id(0)
    per = 8
    lane = iota((K, 128), 1)
    lane8 = iota((8, 128), 1)
    nt = cols // 128

    def field(i):
        return jnp.concatenate([r[pl.ds(i, K, stride=rows), :] for r in (ua_ref, ub_ref)], 1)

    def tiles(a):
        return [a[:, 128 * t : 128 * t + 128] for t in range(nt)]

    def shifted_left(parts, edge, lanes):
        turned = [pltpu.roll(p, 127, 1) for p in parts] + [edge]
        return [jnp.where(lanes == 127, turned[t + 1], turned[t]) for t in range(nt)]

    def shifted_right(parts, edge, lanes):
        turned = [edge] + [pltpu.roll(p, 1, 1) for p in parts]
        return [jnp.where(lanes == 0, turned[t], turned[t + 1]) for t in range(nt)]

    def spread(row):
        return jnp.broadcast_to(row[0:1, :], (K, 128))

    base = step * per
    is_first = step == 0
    is_last = step == rows // per - 1
    before = jnp.where(is_first, up_ref[...], jnp.concatenate([field(jnp.maximum(base - 1, 0)), jnp.broadcast_to(k_ref[pl.ds(jnp.maximum(base - 1, 0), 1), :], (8, cols))], 0))
    after = jnp.where(is_last, dn_ref[...], jnp.concatenate([field(jnp.minimum(base + per, rows - 1)), jnp.broadcast_to(k_ref[pl.ds(jnp.minimum(base + per, rows - 1), 1), :], (8, cols))], 0))
    u_now = field(base)
    k_now = k_ref[pl.ds(base, 1), :]
    flux_before = [
        spread(a) * (b - c)
        for a, b, c in zip(tiles(0.5 * (before[K : K + 1] + k_now)), tiles(before[:K]), tiles(u_now))
    ]
    for n in range(per):
        i = base + n
        if n < per - 1:
            u_next, k_next = field(i + 1), k_ref[pl.ds(i + 1, 1), :]
        else:
            u_next, k_next = after[:K], after[K : K + 1]
        u_t, k_t = tiles(u_now), tiles(k_now)
        flux = [
            spread(a) * (b - c) for a, b, c in zip(tiles(0.5 * (k_now + k_next)), u_t, tiles(u_next))
        ]
        left = pltpu.roll(lf_ref[...], 128 - i, 1)
        right = pltpu.roll(rt_ref[...], 127 - i, 1)
        k_right = shifted_left(k_t, right[K : K + 1], lane8[:1])
        u_right = shifted_left(u_t, right[:K], lane)
        along = [
            spread(0.5 * (a + b)) * (c - d) for a, b, c, d in zip(k_t, k_right, u_t, u_right)
        ]
        entering = spread(0.5 * (left[K : K + 1] + k_t[0])) * (left[:K] - u_t[0])
        along_before = shifted_right(along, entering, lane)
        v_t = tiles(v_ref[pl.ds(i, 1), :])
        for t in range(nt):
            m = jnp.concatenate(
                [u_t[t], flux[t] - flux_before[t], along[t] - along_before[t], spread(v_t[t]) * u_t[t]], 0
            )
            high = m.astype(BF16)
            low = (m - high.astype(F32)).astype(BF16)
            at = n * cols + 128 * t
            mhl_ref[:C, at : at + 128] = high
            mhl_ref[C:, at : at + 128] = low
        u_now, k_now, flux_before = u_next, k_next, flux
    part = lax.dot_general(
        mhl_ref[:C, :], mhl_ref[...], (((1,), (1,)), ((), ())), preferred_element_type=F32
    )

    @pl.when(is_first)
    def _():
        acc_ref[...] = part

    @pl.when(jnp.logical_not(is_first))
    def _():
        acc_ref[...] += part

    @pl.when(is_last)
    def _():
        cross = acc_ref[:, C:]
        gram_ref[...] = (acc_ref[:, :C] + (cross + cross.T)) * scale


def columns_and_gram(u2, conduct, potential, up, down, left, right, scale):
    rows, cols = conduct.shape
    whole = lambda a: pl.BlockSpec(a.shape, lambda s: (0,) * a.ndim)
    args = (u2, u2, conduct, potential, up, down, left, right)
    side = lambda t: pl.BlockSpec((u2.shape[0], 128), lambda s: (0, t))
    return pl.pallas_call(
        lambda *refs: gram_kernel(rows, cols, scale, *refs),
        name="gram",
        grid=(rows // 8,),
        out_shape=[jax.ShapeDtypeStruct((C, C), F32), jax.ShapeDtypeStruct((2 * C, rows * cols), BF16)],
        in_specs=[side(0), side(1)] + [whole(a) for a in args[2:]],
        out_specs=[pl.BlockSpec((C, C), lambda s: (0, 0)), pl.BlockSpec((2 * C, 8 * cols), lambda s: (0, s))],
        scratch_shapes=[pltpu.VMEM((C, 2 * C), F32)],
        compiler_params=pltpu.CompilerParams(vmem_limit_bytes=32 << 20, dimension_semantics=("arbitrary",)),
    )(*args)


def factor(gram):
    blocks = C // NB
    sub = iota((NB, C), 0)
    lane = iota((NB, C), 1)
    shape = (NB, C)
    a = [gram[NB * q : NB * q + NB] for q in range(blocks)]
    e = [jnp.where(lane == sub + NB * q, 1.0, 0.0).astype(F32) for q in range(blocks)]
    upper, inverse = [], []
    for p in range(blocks):
        col = lambda m, j: jnp.broadcast_to(m[:, NB * p + j : NB * p + j + 1], shape)
        row = lambda m, j: jnp.broadcast_to(m[j : j + 1, :], shape)
        cols = [col(a[p], j) for j in range(NB)]
        d = {(i, j): row(cols[j], i) for j in range(NB) for i in range(j + 1)}
        l, x = {}, {}
        for k in range(NB):
            r = lax.rsqrt(d[k, k])
            for j in range(k + 1, NB):
                l[k, j] = d[k, j] * r
            for i in range(k + 1, NB):
                for j in range(i, NB):
                    d[i, j] = d[i, j] - l[k, i] * l[k, j]
            x[k, k] = r
            for j in range(k):
                s = l[j, k] * x[j, j]
                for m in range(j + 1, k):
                    s = s + l[m, k] * x[m, j]
                x[k, j] = -(s * r)

        def combine(parts):
            out = []
            for k in range(NB):
                s = x[k, 0] * parts[0]
                for j in range(1, k + 1):
                    s = s + x[k, j] * parts[j]
                out.append(s)
            return out

        ra = combine([row(a[p], j) for j in range(NB)])
        re = combine([row(e[p], j) for j in range(NB)])
        ua, ue = ra[0], re[0]
        for k in range(1, NB):
            ua = jnp.where(sub == k, ra[k], ua)
            ue = jnp.where(sub == k, re[k], ue)
        upper.append(jnp.where(lane >= sub + NB * p, ua, 0.0))
        inverse.append(ue)
        for q in range(p + 1, blocks):
            c = combine([col(a[q], j) for j in range(NB)])
            sa, se = c[0] * ra[0], c[0] * re[0]
            for k in range(1, NB):
                sa, se = sa + c[k] * ra[k], se + c[k] * re[k]
            a[q], e[q] = a[q] - sa, e[q] - se
    return upper, inverse


def finish_kernel(rows, cols, gram_ref, mhl_ref, out_ref, upper_ref, m_buf, o_buf, x_ref, in_sem, out_sem):
    groups = rows // 8
    wide = 8 * cols
    sides = cols // 128

    def arrive(g):
        span = pl.ds(pl.multiple_of(g * wide, wide), wide)
        return pltpu.make_async_copy(mhl_ref.at[:, span], m_buf.at[:, span], in_sem.at[g])

    def leave(g, t):
        place = out_ref.at[:, pl.ds(pl.multiple_of(g * 8, 8), 8), 128 * t : 128 * t + 128]
        return pltpu.make_async_copy(o_buf.at[g, t].reshape(C, 8, 128), place, out_sem.at[g, t])

    for g in range(groups):
        arrive(g).start()
    upper, inverse = factor(gram_ref[...])
    for p in range(C // NB):
        upper_ref[NB * p : NB * p + NB, :] = upper[p]
    x = jnp.concatenate(inverse, 0)
    high = x.astype(BF16)
    x_ref[:C, :C] = high
    x_ref[:C, C:] = high
    x_ref[C:, :C] = (x - high.astype(F32)).astype(BF16)

    @pl.loop(0, groups)
    def _(g):
        arrive(g).wait()
        for n in range(8):
            m = m_buf[:, pl.ds(pl.multiple_of(g * wide + n * cols, cols), cols)]
            b = jnp.dot(x_ref[:C, :], m, preferred_element_type=F32)
            b = b + jnp.dot(x_ref[C:, :C], m[:C], preferred_element_type=F32)
            for t in range(sides):
                o_buf[g, t, pl.ds(n, C, stride=8), :] = b[:, 128 * t : 128 * t + 128]
        for t in range(sides):
            leave(g, t).start()

    for g in range(groups):
        for t in range(sides):
            leave(g, t).wait()


def finish(gram, mhl, rows, cols):
    full = pl.BlockSpec(memory_space=pltpu.VMEM)
    far = pl.BlockSpec(memory_space=pl.ANY)
    groups = rows // 8
    return pl.pallas_call(
        lambda *refs: finish_kernel(rows, cols, *refs),
        name="finish",
        out_shape=[jax.ShapeDtypeStruct((C, rows, cols), F32), jax.ShapeDtypeStruct((C, C), F32)],
        in_specs=[full, far],
        out_specs=[far, full],
        scratch_shapes=[
            pltpu.VMEM((2 * C, rows * cols), BF16),
            pltpu.VMEM((groups, cols // 128, C * 8, 128), F32),
            pltpu.VMEM((2 * C, 2 * C), BF16),
            pltpu.SemaphoreType.DMA((groups,)),
            pltpu.SemaphoreType.DMA((groups, cols // 128)),
        ],
        compiler_params=pltpu.CompilerParams(vmem_limit_bytes=40 << 20),
    )(gram, mhl)


def butterfly_sum(value):
    rounds = (("gy", 1), ("gy", 2), ("gy", 6), ("gx", 1), ("gx", 3), ("gx", 4), ("gx", 8), ("gx", 28))
    for axis, flip in rounds:
        pairs = [(i, i ^ flip) for i in range(lax.axis_size(axis))]
        value = value + lax.ppermute(value, axis, pairs)
    return value


def on_device(mode_fields, conductance, potential):
    fields, rows, cols = mode_fields.shape
    u2 = mode_fields.reshape(fields * rows, cols)
    top, bottom, left, right = edges(u2, conductance)

    def send(value, axis, forward):
        peers = lax.axis_size(axis)
        up = [(i, i + 1) for i in range(peers - 1)]
        return lax.ppermute(value, axis, up if forward else [(j, i) for i, j in up])

    from_up = send(bottom, "gx", True)
    from_down = send(top, "gx", False)
    from_left = send(right, "gy", True)
    from_right = send(left, "gy", False)
    cells = rows * cols * lax.axis_size("gx") * lax.axis_size("gy")
    gram, mhl = columns_and_gram(u2, conductance, potential, from_up, from_down, from_left, from_right, 1.0 / cells)
    basis_field, scaled_factor = finish(butterfly_sum(gram), mhl, rows, cols)
    return (basis_field, scaled_factor)


def solution(mesh):
    placed = (P(None, "gx", "gy"), P("gx", "gy"), P("gx", "gy"))
    return jax.shard_map(
        on_device, mesh=mesh, in_specs=placed, out_specs=(P(None, "gx", "gy"), P()), check_vma=False
    )
```

```python
import jax
import jax.numpy as jnp
from jax import lax
from jax.experimental import pallas as pl
from jax.experimental.pallas import tpu as pltpu
from jax.sharding import PartitionSpec as P

F32 = jnp.float32
BF16 = jnp.bfloat16
K = 32
C = 128
NB = 8


def iota(shape, dim):
    return lax.broadcasted_iota(jnp.int32, shape, dim)


def edges_kernel(
    rows, cols, u_ref, k_ref, v_ref, top_ref, bottom_ref, left_ref, right_ref, rows_ref, ko_ref, vo_ref, buf, u_sem, c_sem
):
    sides = cols // 128
    groups = rows // 8

    def arrive(g, t):
        return pltpu.make_async_copy(
            u_ref.at[:, 8 * g : 8 * g + 8, 128 * t : 128 * t + 128], buf.at[g, t].reshape(K, 8, 128), u_sem.at[g, t]
        )

    k_copy = pltpu.make_async_copy(k_ref, ko_ref, c_sem.at[0])
    v_copy = pltpu.make_async_copy(v_ref, vo_ref, c_sem.at[1])
    k_copy.start()
    for g in range(groups):
        for t in range(sides):
            arrive(g, t).start()
    v_copy.start()
    k_copy.wait()
    lane = iota((8, 128), 1)
    left = [jnp.zeros((8, 128), F32)] * (K // 8 + 1)
    right = [jnp.zeros((8, 128), F32)] * (K // 8 + 1)
    for i in range(rows):
        g, n = i // 8, i % 8
        if n == 0:
            for t in range(sides):
                arrive(g, t).wait()
        here = lane == i
        parts = [buf[g, t, pl.ds(n, K, stride=8), :] for t in range(sides)]
        for t in range(sides):
            rows_ref[K * i : K * i + K, 128 * t : 128 * t + 128] = parts[t]
        conduct = jnp.broadcast_to(ko_ref[i : i + 1, :], (8, cols))
        for ref, at in ((top_ref, 0), (bottom_ref, rows - 1)):
            if i == at:
                for t in range(sides):
                    ref[:K, 128 * t : 128 * t + 128] = parts[t]
                ref[K:, :] = conduct
        for b in range(K // 8 + 1):
            if b == K // 8:
                first, last = conduct[:, :128], conduct[:, cols - 128 :]
            else:
                first, last = parts[0][8 * b : 8 * b + 8], parts[-1][8 * b : 8 * b + 8]
            left[b] = jnp.where(here, pltpu.roll(first, i, 1) if i else first, left[b])
            right[b] = jnp.where(here, pltpu.roll(last, (i + 1) % 128, 1), right[b])
    for b in range(K // 8 + 1):
        left_ref[8 * b : 8 * b + 8, :] = left[b]
        right_ref[8 * b : 8 * b + 8, :] = right[b]
    v_copy.wait()


def edges(fields, conduct, potential):
    rows, cols = conduct.shape
    far = pl.BlockSpec(memory_space=pltpu.HBM)
    near = pl.BlockSpec(memory_space=pltpu.VMEM)
    sizes = [(K + 8, cols)] * 2 + [(K + 8, 128)] * 2 + [(K * rows, cols)] + [(rows, cols)] * 2
    return pl.pallas_call(
        lambda *refs: edges_kernel(rows, cols, *refs),
        name="edges",
        out_shape=[jax.ShapeDtypeStruct(n, F32) for n in sizes],
        in_specs=[far] * 3,
        out_specs=[near] * 7,
        scratch_shapes=[
            pltpu.VMEM((rows // 8, cols // 128, K * 8, 128), F32),
            pltpu.SemaphoreType.DMA((rows // 8, cols // 128)),
            pltpu.SemaphoreType.DMA((2,)),
        ],
        compiler_params=pltpu.CompilerParams(vmem_limit_bytes=16 << 20),
    )(*[pltpu.with_memory_space_constraint(a, pltpu.HBM) for a in (fields, conduct, potential)])


def gram_kernel(rows, cols, scale, u_ref, k_ref, v_ref, up_ref, dn_ref, lf_ref, rt_ref, gram_ref, mhl_ref, acc_ref):
    per = 8
    wide = per * cols
    lane = iota((K, 128), 1)
    lane8 = iota((8, 128), 1)
    nt = cols // 128

    def field(i):
        return u_ref[pl.ds(pl.multiple_of(i * K, K), K), :]

    def tiles(a):
        return [a[:, 128 * t : 128 * t + 128] for t in range(nt)]

    def shifted_left(parts, edge, lanes):
        turned = [pltpu.roll(p, 127, 1) for p in parts] + [edge]
        return [jnp.where(lanes == 127, turned[t + 1], turned[t]) for t in range(nt)]

    def shifted_right(parts, edge, lanes):
        turned = [edge] + [pltpu.roll(p, 1, 1) for p in parts]
        return [jnp.where(lanes == 0, turned[t], turned[t + 1]) for t in range(nt)]

    def spread(row):
        return jnp.broadcast_to(row[0:1, :], (K, 128))

    acc_ref[...] = jnp.zeros_like(acc_ref)

    @pl.loop(0, rows // per)
    def _(step):
        base = step * per
        is_first = step == 0
        is_last = step == rows // per - 1
        i_before = jnp.maximum(base - 1, 0)
        i_after = jnp.minimum(base + per, rows - 1)
        u_before = jnp.where(is_first, up_ref[:K], field(i_before))
        k_before = jnp.where(is_first, up_ref[K : K + 1], k_ref[pl.ds(i_before, 1), :])
        u_after = jnp.where(is_last, dn_ref[:K], field(i_after))
        k_after = jnp.where(is_last, dn_ref[K : K + 1], k_ref[pl.ds(i_after, 1), :])
        u_now = field(base)
        k_now = k_ref[pl.ds(base, 1), :]
        flux_before = [
            spread(a) * (b - c) for a, b, c in zip(tiles(0.5 * (k_before + k_now)), tiles(u_before), tiles(u_now))
        ]
        for n in range(per):
            i = base + n
            if n < per - 1:
                u_next, k_next = field(i + 1), k_ref[pl.ds(i + 1, 1), :]
            else:
                u_next, k_next = u_after, k_after
            u_t, k_t = tiles(u_now), tiles(k_now)
            flux = [spread(a) * (b - c) for a, b, c in zip(tiles(0.5 * (k_now + k_next)), u_t, tiles(u_next))]
            left = pltpu.roll(lf_ref[...], 128 - i, 1)
            right = pltpu.roll(rt_ref[...], 127 - i, 1)
            k_right = shifted_left(k_t, right[K : K + 1], lane8[:1])
            u_right = shifted_left(u_t, right[:K], lane)
            along = [spread(0.5 * (a + b)) * (c - d) for a, b, c, d in zip(k_t, k_right, u_t, u_right)]
            entering = spread(0.5 * (left[K : K + 1] + k_t[0])) * (left[:K] - u_t[0])
            along_before = shifted_right(along, entering, lane)
            v_t = tiles(v_ref[pl.ds(i, 1), :])
            for t in range(nt):
                m = jnp.concatenate(
                    [u_t[t], flux[t] - flux_before[t], along[t] - along_before[t], spread(v_t[t]) * u_t[t]], 0
                )
                high = m.astype(BF16)
                low = (m - high.astype(F32)).astype(BF16)
                at = pl.ds(pl.multiple_of(step * wide + n * cols + 128 * t, 128), 128)
                mhl_ref[:C, at] = high
                mhl_ref[C:, at] = low
            u_now, k_now, flux_before = u_next, k_next, flux
        span = pl.ds(pl.multiple_of(step * wide, wide), wide)
        acc_ref[...] += lax.dot_general(
            mhl_ref[:C, span], mhl_ref[:, span], (((1,), (1,)), ((), ())), preferred_element_type=F32
        )

    cross = acc_ref[:, C:]
    total = (acc_ref[:, :C] + (cross + cross.T)) * scale
    lane32 = iota((32, C), 1)
    lane16 = iota((16, C), 1)
    gram_ref[:32, :] = total[:32]
    gram_ref[32:64, :] = jnp.where(lane32 >= 32, total[32:64], pltpu.roll(total[96:], 32, 1))
    gram_ref[64:, :] = jnp.where(lane16 >= 64, total[64:80], pltpu.roll(total[80:96], 64, 1))


def unpacked(packed):
    lane32 = iota((32, C), 1)
    lane16 = iota((16, C), 1)
    middle, tail = packed[32:64], packed[64:]
    upper = jnp.concatenate(
        [
            packed[:32],
            jnp.where(lane32 >= 32, middle, 0.0),
            jnp.where(lane16 >= 64, tail, 0.0),
            jnp.where(lane16 >= 64, pltpu.roll(tail, 64, 1), 0.0),
            jnp.where(lane32 >= 96, pltpu.roll(middle, 96, 1), 0.0),
        ],
        0,
    )
    return jnp.where(iota((C, C), 1) // 32 >= iota((C, C), 0) // 32, upper, upper.T)


def columns_and_gram(u_rows, conduct, potential, up, down, left, right, scale):
    rows, cols = conduct.shape
    near = pl.BlockSpec(memory_space=pltpu.VMEM)
    args = (u_rows, conduct, potential, up, down, left, right)
    return pl.pallas_call(
        lambda *refs: gram_kernel(rows, cols, scale, *refs),
        name="gram",
        out_shape=[jax.ShapeDtypeStruct((80, C), F32), jax.ShapeDtypeStruct((2 * C, rows * cols), BF16)],
        in_specs=[near] * len(args),
        out_specs=[near] * 2,
        scratch_shapes=[pltpu.VMEM((C, 2 * C), F32)],
        compiler_params=pltpu.CompilerParams(vmem_limit_bytes=32 << 20),
    )(*args)


def factor(gram):
    blocks = C // NB
    sub = iota((NB, C), 0)
    lane = iota((NB, C), 1)
    shape = (NB, C)
    a = [gram[NB * q : NB * q + NB] for q in range(blocks)]
    e = [jnp.where(lane == sub + NB * q, 1.0, 0.0).astype(F32) for q in range(blocks)]
    upper, inverse = [], []
    for p in range(blocks):
        col = lambda m, j: jnp.broadcast_to(m[:, NB * p + j : NB * p + j + 1], shape)
        row = lambda m, j: jnp.broadcast_to(m[j : j + 1, :], shape)
        cols = [col(a[p], j) for j in range(NB)]
        d = {(i, j): row(cols[j], i) for j in range(NB) for i in range(j + 1)}
        l, x = {}, {}
        for k in range(NB):
            r = lax.rsqrt(d[k, k])
            for j in range(k + 1, NB):
                l[k, j] = d[k, j] * r
            for i in range(k + 1, NB):
                for j in range(i, NB):
                    d[i, j] = d[i, j] - l[k, i] * l[k, j]
            x[k, k] = r
            for j in range(k):
                s = l[j, k] * x[j, j]
                for m in range(j + 1, k):
                    s = s + l[m, k] * x[m, j]
                x[k, j] = -(s * r)

        def combine(parts):
            out = []
            for k in range(NB):
                s = x[k, 0] * parts[0]
                for j in range(1, k + 1):
                    s = s + x[k, j] * parts[j]
                out.append(s)
            return out

        ra = combine([row(a[p], j) for j in range(NB)])
        re = combine([row(e[p], j) for j in range(NB)])
        ua, ue = ra[0], re[0]
        for k in range(1, NB):
            ua = jnp.where(sub == k, ra[k], ua)
            ue = jnp.where(sub == k, re[k], ue)
        upper.append(jnp.where(lane >= sub + NB * p, ua, 0.0))
        inverse.append(ue)
        for q in range(p + 1, blocks):
            c = combine([col(a[q], j) for j in range(NB)])
            sa, se = c[0] * ra[0], c[0] * re[0]
            for k in range(1, NB):
                sa, se = sa + c[k] * ra[k], se + c[k] * re[k]
            a[q], e[q] = a[q] - sa, e[q] - se
    return upper, inverse


def finish_kernel(rows, cols, gram_ref, mhl_ref, out_ref, upper_ref, o_buf, x_ref, out_sem):
    groups = rows // 8
    wide = 8 * cols
    sides = cols // 128

    def leave(g, t):
        place = out_ref.at[:, pl.ds(pl.multiple_of(g * 8, 8), 8), 128 * t : 128 * t + 128]
        return pltpu.make_async_copy(o_buf.at[g, t].reshape(C, 8, 128), place, out_sem.at[g, t])

    upper, inverse = factor(unpacked(gram_ref[...]))
    for p in range(C // NB):
        upper_ref[NB * p : NB * p + NB, :] = upper[p]
    x = jnp.concatenate(inverse, 0)
    high = x.astype(BF16)
    x_ref[:C, :C] = high
    x_ref[:C, C:] = high
    x_ref[C:, :C] = (x - high.astype(F32)).astype(BF16)

    @pl.loop(0, groups)
    def _(g):
        for n in range(8):
            m = mhl_ref[:, pl.ds(pl.multiple_of(g * wide + n * cols, cols), cols)]
            b = jnp.dot(x_ref[:C, :], m, preferred_element_type=F32)
            b = b + jnp.dot(x_ref[C:, :C], m[:C], preferred_element_type=F32)
            for t in range(sides):
                o_buf[g, t, pl.ds(n, C, stride=8), :] = b[:, 128 * t : 128 * t + 128]
        for t in range(sides):
            leave(g, t).start()

    for g in range(groups):
        for t in range(sides):
            leave(g, t).wait()


def finish(gram, mhl, rows, cols):
    near = pl.BlockSpec(memory_space=pltpu.VMEM)
    far = pl.BlockSpec(memory_space=pl.ANY)
    groups = rows // 8
    return pl.pallas_call(
        lambda *refs: finish_kernel(rows, cols, *refs),
        name="finish",
        out_shape=[jax.ShapeDtypeStruct((C, rows, cols), F32), jax.ShapeDtypeStruct((C, C), F32)],
        in_specs=[near, near],
        out_specs=[far, near],
        scratch_shapes=[
            pltpu.VMEM((groups, cols // 128, C * 8, 128), F32),
            pltpu.VMEM((2 * C, 2 * C), BF16),
            pltpu.SemaphoreType.DMA((groups, cols // 128)),
        ],
        compiler_params=pltpu.CompilerParams(vmem_limit_bytes=40 << 20),
    )(gram, mhl)


def exchanged(value, flips):
    across = lax.axis_size("gy")
    pairs = []
    for i in range(lax.axis_size("gx")):
        for j in range(across):
            along_x, along_y = flips[j % 2]
            pairs.append((i * across + j, (i ^ along_x) * across + (j ^ along_y)))
    return lax.ppermute(value, ("gx", "gy"), pairs)


def sum_over_devices(value):
    value = value + exchanged(value, ((0, 1), (0, 1)))
    along_x, along_y, along_z = ((1, 0), (2, 0), (3, 0)), ((0, 2), (0, 4), (0, 6)), ((4, 0), (8, 0), (12, 0))
    for group in (tuple(zip(along_x, along_y)), tuple(zip(along_y, along_x)), tuple(zip(along_z, along_z))):
        second = exchanged(value, group[1])
        first, third = exchanged(value, group[0]), exchanged(value, group[2])
        value = (value + first) + (second + third)
    return value + exchanged(value, ((28, 0), (28, 0)))


def on_device(mode_fields, conductance, potential):
    fields, rows, cols = mode_fields.shape
    top, bottom, left, right, u_rows, conduct, potent = edges(mode_fields, conductance, potential)

    def send(value, axis, forward):
        peers = lax.axis_size(axis)
        up = [(i, i + 1) for i in range(peers - 1)]
        return lax.ppermute(value, axis, up if forward else [(j, i) for i, j in up])

    from_up = send(bottom, "gx", True)
    from_down = send(top, "gx", False)
    from_left = send(right, "gy", True)
    from_right = send(left, "gy", False)
    cells = rows * cols * lax.axis_size("gx") * lax.axis_size("gy")
    gram, mhl = columns_and_gram(u_rows, conduct, potent, from_up, from_down, from_left, from_right, 1.0 / cells)
    basis_field, scaled_factor = finish(sum_over_devices(gram), mhl, rows, cols)
    return (basis_field, scaled_factor)


def solution(mesh):
    placed = (P(None, "gx", "gy"), P("gx", "gy"), P("gx", "gy"))
    return jax.shard_map(
        on_device, mesh=mesh, in_specs=placed, out_specs=(P(None, "gx", "gy"), P()), check_vma=False
    )
```

```python
import jax
import jax.numpy as jnp
from jax import lax
from jax.experimental import pallas as pl
from jax.experimental.pallas import tpu as pltpu
from jax.sharding import PartitionSpec as P

F32 = jnp.float32
BF16 = jnp.bfloat16
K = 32
C = 128
NB = 8


def iota(shape, dim):
    return lax.broadcasted_iota(jnp.int32, shape, dim)


def edges_kernel(
    rows, cols, u_ref, k_ref, v_ref, top_ref, bottom_ref, left_ref, right_ref, rows_ref, ko_ref, vo_ref, buf, u_sem, c_sem
):
    sides = cols // 128
    groups = rows // 8

    def arrive(g, t):
        return pltpu.make_async_copy(
            u_ref.at[:, pl.ds(pl.multiple_of(8 * g, 8), 8), 128 * t : 128 * t + 128], buf.at[g, t].reshape(K, 8, 128), u_sem.at[g, t]
        )

    k_copy = pltpu.make_async_copy(k_ref, ko_ref, c_sem.at[0])
    v_copy = pltpu.make_async_copy(v_ref, vo_ref, c_sem.at[1])
    k_copy.start()
    for g in range(groups):
        for t in range(sides):
            arrive(g, t).start()
    v_copy.start()
    k_copy.wait()
    lane = iota((8, 128), 1)
    left = [jnp.zeros((8, 128), F32)] * (K // 8 + 1)
    right = [jnp.zeros((8, 128), F32)] * (K // 8 + 1)
    for i in range(rows):
        g, n = i // 8, i % 8
        if n == 0:
            for t in range(sides):
                arrive(g, t).wait()
        here = lane == i
        parts = [buf[g, t, pl.ds(n, K, stride=8), :] for t in range(sides)]
        for t in range(sides):
            rows_ref[K * i : K * i + K, 128 * t : 128 * t + 128] = parts[t]
        conduct = jnp.broadcast_to(ko_ref[i : i + 1, :], (8, cols))
        for ref, at in ((top_ref, 0), (bottom_ref, rows - 1)):
            if i == at:
                for t in range(sides):
                    ref[:K, 128 * t : 128 * t + 128] = parts[t]
                ref[K:, :] = conduct
        for b in range(K // 8 + 1):
            if b == K // 8:
                first, last = conduct[:, :128], conduct[:, cols - 128 :]
            else:
                first, last = parts[0][8 * b : 8 * b + 8], parts[-1][8 * b : 8 * b + 8]
            left[b] = jnp.where(here, pltpu.roll(first, i, 1) if i else first, left[b])
            right[b] = jnp.where(here, pltpu.roll(last, (i + 1) % 128, 1), right[b])
    for b in range(K // 8 + 1):
        left_ref[8 * b : 8 * b + 8, :] = left[b]
        right_ref[8 * b : 8 * b + 8, :] = right[b]
    v_copy.wait()


def edges(fields, conduct, potential):
    rows, cols = conduct.shape
    far = pl.BlockSpec(memory_space=pltpu.HBM)
    near = pl.BlockSpec(memory_space=pltpu.VMEM)
    sizes = [(K + 8, cols)] * 2 + [(K + 8, 128)] * 2 + [(K * rows, cols)] + [(rows, cols)] * 2
    return pl.pallas_call(
        lambda *refs: edges_kernel(rows, cols, *refs),
        name="edges",
        out_shape=[jax.ShapeDtypeStruct(n, F32) for n in sizes],
        in_specs=[far] * 3,
        out_specs=[near] * 7,
        scratch_shapes=[
            pltpu.VMEM((rows // 8, cols // 128, K * 8, 128), F32),
            pltpu.SemaphoreType.DMA((rows // 8, cols // 128)),
            pltpu.SemaphoreType.DMA((2,)),
        ],
        compiler_params=pltpu.CompilerParams(vmem_limit_bytes=16 << 20),
    )(*[pltpu.with_memory_space_constraint(a, pltpu.HBM) for a in (fields, conduct, potential)])


def gram_kernel(rows, cols, scale, u_ref, k_ref, v_ref, up_ref, dn_ref, lf_ref, rt_ref, gram_ref, mhl_ref, acc_ref):
    per = 8
    wide = per * cols
    lane = iota((K, 128), 1)
    lane8 = iota((8, 128), 1)
    nt = cols // 128

    def field(i):
        return u_ref[pl.ds(pl.multiple_of(i * K, K), K), :]

    def tiles(a):
        return [a[:, 128 * t : 128 * t + 128] for t in range(nt)]

    def shifted_left(parts, edge, lanes):
        turned = [pltpu.roll(p, 127, 1) for p in parts] + [edge]
        return [jnp.where(lanes == 127, turned[t + 1], turned[t]) for t in range(nt)]

    def shifted_right(parts, edge, lanes):
        turned = [edge] + [pltpu.roll(p, 1, 1) for p in parts]
        return [jnp.where(lanes == 0, turned[t], turned[t + 1]) for t in range(nt)]

    def spread(row):
        return jnp.broadcast_to(row[0:1, :], (K, 128))

    acc_ref[...] = jnp.zeros_like(acc_ref)

    @pl.loop(0, rows // per, unroll=True)
    def _(step):
        base = step * per
        is_first = step == 0
        is_last = step == rows // per - 1
        i_before = jnp.maximum(base - 1, 0)
        i_after = jnp.minimum(base + per, rows - 1)
        u_before = jnp.where(is_first, up_ref[:K], field(i_before))
        k_before = jnp.where(is_first, up_ref[K : K + 1], k_ref[pl.ds(i_before, 1), :])
        u_after = jnp.where(is_last, dn_ref[:K], field(i_after))
        k_after = jnp.where(is_last, dn_ref[K : K + 1], k_ref[pl.ds(i_after, 1), :])
        u_now = field(base)
        k_now = k_ref[pl.ds(base, 1), :]
        flux_before = [
            spread(a) * (b - c) for a, b, c in zip(tiles(0.5 * (k_before + k_now)), tiles(u_before), tiles(u_now))
        ]
        for n in range(per):
            i = base + n
            if n < per - 1:
                u_next, k_next = field(i + 1), k_ref[pl.ds(i + 1, 1), :]
            else:
                u_next, k_next = u_after, k_after
            u_t, k_t = tiles(u_now), tiles(k_now)
            flux = [spread(a) * (b - c) for a, b, c in zip(tiles(0.5 * (k_now + k_next)), u_t, tiles(u_next))]
            left = pltpu.roll(lf_ref[...], 128 - i, 1)
            right = pltpu.roll(rt_ref[...], 127 - i, 1)
            k_right = shifted_left(k_t, right[K : K + 1], lane8[:1])
            u_right = shifted_left(u_t, right[:K], lane)
            along = [spread(0.5 * (a + b)) * (c - d) for a, b, c, d in zip(k_t, k_right, u_t, u_right)]
            entering = spread(0.5 * (left[K : K + 1] + k_t[0])) * (left[:K] - u_t[0])
            along_before = shifted_right(along, entering, lane)
            v_t = tiles(v_ref[pl.ds(i, 1), :])
            for t in range(nt):
                m = jnp.concatenate(
                    [u_t[t], flux[t] - flux_before[t], along[t] - along_before[t], spread(v_t[t]) * u_t[t]], 0
                )
                high = m.astype(BF16)
                low = (m - high.astype(F32)).astype(BF16)
                at = pl.ds(pl.multiple_of(step * wide + n * cols + 128 * t, 128), 128)
                mhl_ref[:C, at] = high
                mhl_ref[C:, at] = low
            u_now, k_now, flux_before = u_next, k_next, flux
        span = pl.ds(pl.multiple_of(step * wide, wide), wide)
        acc_ref[...] += lax.dot_general(
            mhl_ref[:C, span], mhl_ref[:, span], (((1,), (1,)), ((), ())), preferred_element_type=F32
        )

    cross = acc_ref[:, C:]
    total = (acc_ref[:, :C] + (cross + cross.T)) * scale
    lane32 = iota((32, C), 1)
    lane16 = iota((16, C), 1)
    gram_ref[:32, :] = total[:32]
    gram_ref[32:64, :] = jnp.where(lane32 >= 32, total[32:64], pltpu.roll(total[96:], 32, 1))
    gram_ref[64:, :] = jnp.where(lane16 >= 64, total[64:80], pltpu.roll(total[80:96], 64, 1))


def unpacked(packed):
    lane32 = iota((32, C), 1)
    lane16 = iota((16, C), 1)
    middle, tail = packed[32:64], packed[64:]
    upper = jnp.concatenate(
        [
            packed[:32],
            jnp.where(lane32 >= 32, middle, 0.0),
            jnp.where(lane16 >= 64, tail, 0.0),
            jnp.where(lane16 >= 64, pltpu.roll(tail, 64, 1), 0.0),
            jnp.where(lane32 >= 96, pltpu.roll(middle, 96, 1), 0.0),
        ],
        0,
    )
    return jnp.where(iota((C, C), 1) // 32 >= iota((C, C), 0) // 32, upper, upper.T)


def columns_and_gram(u_rows, conduct, potential, up, down, left, right, scale):
    rows, cols = conduct.shape
    near = pl.BlockSpec(memory_space=pltpu.VMEM)
    args = (u_rows, conduct, potential, up, down, left, right)
    return pl.pallas_call(
        lambda *refs: gram_kernel(rows, cols, scale, *refs),
        name="gram",
        out_shape=[jax.ShapeDtypeStruct((80, C), F32), jax.ShapeDtypeStruct((2 * C, rows * cols), BF16)],
        in_specs=[near] * len(args),
        out_specs=[near] * 2,
        scratch_shapes=[pltpu.VMEM((C, 2 * C), F32)],
        compiler_params=pltpu.CompilerParams(vmem_limit_bytes=32 << 20),
    )(*args)


def factor(gram, after_panel):
    blocks = C // NB
    sub = iota((NB, C), 0)
    lane = iota((NB, C), 1)
    shape = (NB, C)
    a = [gram[NB * q : NB * q + NB] for q in range(blocks)]
    e = [jnp.where(lane == sub + NB * q, 1.0, 0.0).astype(F32) for q in range(blocks)]
    upper, inverse = [], []
    for p in range(blocks):
        col = lambda m, j: jnp.broadcast_to(m[:, NB * p + j : NB * p + j + 1], shape)
        row = lambda m, j: jnp.broadcast_to(m[j : j + 1, :], shape)
        cols = [col(a[p], j) for j in range(NB)]
        d = {(i, j): row(cols[j], i) for j in range(NB) for i in range(j + 1)}
        l, x = {}, {}
        for k in range(NB):
            r = lax.rsqrt(d[k, k])
            for j in range(k + 1, NB):
                l[k, j] = d[k, j] * r
            for i in range(k + 1, NB):
                for j in range(i, NB):
                    d[i, j] = d[i, j] - l[k, i] * l[k, j]
            x[k, k] = r
            for j in range(k):
                s = l[j, k] * x[j, j]
                for m in range(j + 1, k):
                    s = s + l[m, k] * x[m, j]
                x[k, j] = -(s * r)

        def combine(parts):
            out = []
            for k in range(NB):
                s = x[k, 0] * parts[0]
                for j in range(1, k + 1):
                    s = s + x[k, j] * parts[j]
                out.append(s)
            return out

        def solved(parts):
            out = []
            for j in range(NB):
                s = x[j, j] * parts[j]
                for k in range(j + 1, NB):
                    s = s + x[k, j] * parts[k]
                out.append(s)
            return out

        ra = combine([row(a[p], j) for j in range(NB)])
        re = combine([row(e[p], j) for j in range(NB)])
        ua, ue = ra[0], re[0]
        for k in range(1, NB):
            ua = jnp.where(sub == k, ra[k], ua)
            ue = jnp.where(sub == k, re[k], ue)
        upper.append(jnp.where(lane >= sub + NB * p, ua, 0.0))
        inverse.append(ue)
        wa, we = solved(ra), solved(re)
        for q in range(p + 1, blocks):
            c = [col(a[q], j) for j in range(NB)]
            sa, se = c[0] * wa[0], c[0] * we[0]
            for k in range(1, NB):
                sa, se = sa + c[k] * wa[k], se + c[k] * we[k]
            a[q], e[q] = a[q] - sa, e[q] - se
        after_panel(p, inverse)
    return upper, inverse


def finish_kernel(rows, cols, gram_ref, mhl_ref, out_ref, upper_ref, o_buf, xt_ref, xb_ref, out_sem):
    groups = rows // 8
    sides = cols // 128
    half = C // 2
    panels = C // NB

    def leave(g, t, part):
        place = out_ref.at[half * part : half * part + half, pl.ds(pl.multiple_of(8 * g, 8), 8), 128 * t : 128 * t + 128]
        source = o_buf.at[g, t, 8 * half * part : 8 * half * (part + 1)].reshape(half, 8, 128)
        return pltpu.make_async_copy(source, place, out_sem.at[g, t, part])

    def split(x):
        high = x.astype(BF16)
        low = (x - high.astype(F32)).astype(BF16)
        return jnp.concatenate([jnp.concatenate([high, high], 1), jnp.concatenate([low, jnp.zeros_like(low)], 1)], 0)

    def apply(g, part, left, depth):
        for n in range(8):
            at = pl.ds(pl.multiple_of((8 * g + n) * cols, cols), cols)
            high, low = mhl_ref[:depth, at], mhl_ref[C : C + depth, at]
            b = jnp.dot(left[...], jnp.concatenate([high, low], 0), preferred_element_type=F32)
            b = b[:half] + b[half:]
            for t in range(sides):
                o_buf[g, t, pl.ds(8 * half * part + n, half, stride=8), :] = b[:, 128 * t : 128 * t + 128]
        for t in range(sides):
            leave(g, t, part).start()

    top = []

    def after_panel(p, inverse):
        if p == panels // 2 - 1:
            xt_ref[...] = split(jnp.concatenate(inverse, 0)[:, :half])
        later = panels - panels // 2
        if p >= panels // 2:
            step = p - panels // 2
            for g in range(groups * step // later, groups * (step + 1) // later):
                apply(g, 0, xt_ref, half)

    upper, inverse = factor(unpacked(gram_ref[...]), after_panel)
    for p in range(panels):
        upper_ref[NB * p : NB * p + NB, :] = upper[p]
    xb_ref[...] = split(jnp.concatenate(inverse[panels // 2 :], 0))
    lax.fori_loop(0, groups, lambda g, c: (apply(g, 1, xb_ref, C), c)[1], 0, unroll=4)
    for g in range(groups):
        for t in range(sides):
            for part in range(2):
                leave(g, t, part).wait()


def finish(gram, mhl, rows, cols):
    near = pl.BlockSpec(memory_space=pltpu.VMEM)
    far = pl.BlockSpec(memory_space=pl.ANY)
    groups = rows // 8
    return pl.pallas_call(
        lambda *refs: finish_kernel(rows, cols, *refs),
        name="finish",
        out_shape=[jax.ShapeDtypeStruct((C, rows, cols), F32), jax.ShapeDtypeStruct((C, C), F32)],
        in_specs=[near, near],
        out_specs=[far, near],
        scratch_shapes=[
            pltpu.VMEM((groups, cols // 128, C * 8, 128), F32),
            pltpu.VMEM((C, C), BF16),
            pltpu.VMEM((C, 2 * C), BF16),
            pltpu.SemaphoreType.DMA((groups, cols // 128, 2)),
        ],
        compiler_params=pltpu.CompilerParams(vmem_limit_bytes=40 << 20),
    )(gram, mhl)


def exchanged(value, flips):
    across = lax.axis_size("gy")
    pairs = []
    for i in range(lax.axis_size("gx")):
        for j in range(across):
            along_x, along_y = flips[j % 2]
            pairs.append((i * across + j, (i ^ along_x) * across + (j ^ along_y)))
    return lax.ppermute(value, ("gx", "gy"), pairs)


def sum_over_devices(value):
    value = value + exchanged(value, ((0, 1), (0, 1)))
    along_x, along_y, along_z = ((1, 0), (2, 0), (3, 0)), ((0, 2), (0, 4), (0, 6)), ((4, 0), (8, 0), (12, 0))
    for group in (tuple(zip(along_x, along_y)), tuple(zip(along_y, along_x)), tuple(zip(along_z, along_z))):
        second = exchanged(value, group[1])
        first, third = exchanged(value, group[0]), exchanged(value, group[2])
        value = (value + first) + (second + third)
    return value + exchanged(value, ((28, 0), (28, 0)))


def on_device(mode_fields, conductance, potential):
    fields, rows, cols = mode_fields.shape
    top, bottom, left, right, u_rows, conduct, potent = edges(mode_fields, conductance, potential)

    def send(value, axis, forward):
        peers = lax.axis_size(axis)
        up = [(i, i + 1) for i in range(peers - 1)]
        return lax.ppermute(value, axis, up if forward else [(j, i) for i, j in up])

    from_up = send(bottom, "gx", True)
    from_down = send(top, "gx", False)
    from_left = send(right, "gy", True)
    from_right = send(left, "gy", False)
    cells = rows * cols * lax.axis_size("gx") * lax.axis_size("gy")
    gram, mhl = columns_and_gram(u_rows, conduct, potent, from_up, from_down, from_left, from_right, 1.0 / cells)
    basis_field, scaled_factor = finish(sum_over_devices(gram), mhl, rows, cols)
    return (basis_field, scaled_factor)


def solution(mesh):
    placed = (P(None, "gx", "gy"), P("gx", "gy"), P("gx", "gy"))
    return jax.shard_map(
        on_device, mesh=mesh, in_specs=placed, out_specs=(P(None, "gx", "gy"), P()), check_vma=False
    )
```

```python
import jax
import jax.numpy as jnp
from jax import lax
from jax.experimental import pallas as pl
from jax.experimental.pallas import tpu as pltpu
from jax.sharding import PartitionSpec as P

F32 = jnp.float32
BF16 = jnp.bfloat16
K = 32
C = 128
NB = 8


def iota(shape, dim):
    return lax.broadcasted_iota(jnp.int32, shape, dim)


def edges_kernel(
    rows, cols, u_ref, k_ref, v_ref, x1_ref, x2_ref, y1_ref, y2_ref, rows_ref, ko_ref, vo_ref, buf, u_sem, c_sem
):
    sides = cols // 128
    groups = rows // 8

    def arrive(g, t):
        return pltpu.make_async_copy(
            u_ref.at[:, pl.ds(pl.multiple_of(8 * g, 8), 8), 128 * t : 128 * t + 128], buf.at[g, t].reshape(K, 8, 128), u_sem.at[g, t]
        )

    even_x = lax.axis_index("gx") % 2 == 0
    even_y = lax.axis_index("gy") % 2 == 0
    k_copy = pltpu.make_async_copy(k_ref, ko_ref, c_sem.at[0])
    v_copy = pltpu.make_async_copy(v_ref, vo_ref, c_sem.at[1])
    k_copy.start()
    for g in range(groups):
        for t in range(sides):
            arrive(g, t).start()
    v_copy.start()
    k_copy.wait()
    lane = iota((8, 128), 1)
    left = [jnp.zeros((8, 128), F32)] * (K // 8 + 1)
    right = [jnp.zeros((8, 128), F32)] * (K // 8 + 1)
    for i in range(rows):
        g, n = i // 8, i % 8
        if n == 0:
            for t in range(sides):
                arrive(g, t).wait()
        here = lane == i
        parts = [buf[g, t, pl.ds(n, K, stride=8), :] for t in range(sides)]
        for t in range(sides):
            rows_ref[K * i : K * i + K, 128 * t : 128 * t + 128] = parts[t]
        conduct = jnp.broadcast_to(ko_ref[i : i + 1, :], (8, cols))
        if i == 0:
            top = jnp.concatenate([jnp.concatenate(parts, 1), conduct], 0)
        if i == rows - 1:
            bottom = jnp.concatenate([jnp.concatenate(parts, 1), conduct], 0)
        for b in range(K // 8 + 1):
            if b == K // 8:
                first, last = conduct[:, :128], conduct[:, cols - 128 :]
            else:
                first, last = parts[0][8 * b : 8 * b + 8], parts[-1][8 * b : 8 * b + 8]
            left[b] = jnp.where(here, pltpu.roll(first, i, 1) if i else first, left[b])
            right[b] = jnp.where(here, pltpu.roll(last, (i + 1) % 128, 1), right[b])
    for b in range(K // 8 + 1):
        y1_ref[8 * b : 8 * b + 8, :] = jnp.where(even_y, right[b], left[b])
        y2_ref[8 * b : 8 * b + 8, :] = jnp.where(even_y, left[b], right[b])
    x1_ref[...] = jnp.where(even_x, bottom, top)
    x2_ref[...] = jnp.where(even_x, top, bottom)
    v_copy.wait()


def edges(fields, conduct, potential):
    rows, cols = conduct.shape
    far = pl.BlockSpec(memory_space=pltpu.HBM)
    near = pl.BlockSpec(memory_space=pltpu.VMEM)
    sizes = [(K + 8, cols)] * 2 + [(K + 8, 128)] * 2 + [(K * rows, cols)] + [(rows, cols)] * 2
    return pl.pallas_call(
        lambda *refs: edges_kernel(rows, cols, *refs),
        name="edges",
        out_shape=[jax.ShapeDtypeStruct(n, F32) for n in sizes],
        in_specs=[far] * 3,
        out_specs=[near] * 7,
        scratch_shapes=[
            pltpu.VMEM((rows // 8, cols // 128, K * 8, 128), F32),
            pltpu.SemaphoreType.DMA((rows // 8, cols // 128)),
            pltpu.SemaphoreType.DMA((2,)),
        ],
        compiler_params=pltpu.CompilerParams(vmem_limit_bytes=16 << 20),
    )(*[pltpu.with_memory_space_constraint(a, pltpu.HBM) for a in (fields, conduct, potential)])


def gram_kernel(
    rows, cols, places, scale, u_ref, k_ref, v_ref, x1_ref, x2_ref, y1_ref, y2_ref, gram_ref, mhl_ref, acc_ref, lf_ref, rt_ref
):
    per = 8
    wide = per * cols
    lane = iota((K, 128), 1)
    lane8 = iota((8, 128), 1)
    nt = cols // 128

    def field(i):
        return u_ref[pl.ds(pl.multiple_of(i * K, K), K), :]

    def tiles(a):
        return [a[:, 128 * t : 128 * t + 128] for t in range(nt)]

    def shifted_left(parts, edge, lanes):
        turned = [pltpu.roll(p, 127, 1) for p in parts] + [edge]
        return [jnp.where(lanes == 127, turned[t + 1], turned[t]) for t in range(nt)]

    def shifted_right(parts, edge, lanes):
        turned = [edge] + [pltpu.roll(p, 1, 1) for p in parts]
        return [jnp.where(lanes == 0, turned[t], turned[t + 1]) for t in range(nt)]

    def spread(row):
        return jnp.broadcast_to(row[0:1, :], (K, 128))

    def from_neighbours(axis, first, second):
        at, last = lax.axis_index(axis), places[axis] - 1
        even = at % 2 == 0
        before = jnp.where(at == 0, 0.0, jnp.where(even, second, first))
        return before, jnp.where(at == last, 0.0, jnp.where(even, first, second))

    up, down = from_neighbours("gx", x1_ref[...], x2_ref[...])
    lf_ref[...], rt_ref[...] = from_neighbours("gy", y1_ref[...], y2_ref[...])
    acc_ref[...] = jnp.zeros_like(acc_ref)

    @pl.loop(0, rows // per, unroll=True)
    def _(step):
        base = step * per
        is_first = step == 0
        is_last = step == rows // per - 1
        i_before = jnp.maximum(base - 1, 0)
        i_after = jnp.minimum(base + per, rows - 1)
        u_before = jnp.where(is_first, up[:K], field(i_before))
        k_before = jnp.where(is_first, up[K : K + 1], k_ref[pl.ds(i_before, 1), :])
        u_after = jnp.where(is_last, down[:K], field(i_after))
        k_after = jnp.where(is_last, down[K : K + 1], k_ref[pl.ds(i_after, 1), :])
        u_now = field(base)
        k_now = k_ref[pl.ds(base, 1), :]
        flux_before = [
            spread(a) * (b - c) for a, b, c in zip(tiles(0.5 * (k_before + k_now)), tiles(u_before), tiles(u_now))
        ]
        for n in range(per):
            i = base + n
            if n < per - 1:
                u_next, k_next = field(i + 1), k_ref[pl.ds(i + 1, 1), :]
            else:
                u_next, k_next = u_after, k_after
            u_t, k_t = tiles(u_now), tiles(k_now)
            flux = [spread(a) * (b - c) for a, b, c in zip(tiles(0.5 * (k_now + k_next)), u_t, tiles(u_next))]
            left = pltpu.roll(lf_ref[...], 128 - i, 1)
            right = pltpu.roll(rt_ref[...], 127 - i, 1)
            k_right = shifted_left(k_t, right[K : K + 1], lane8[:1])
            u_right = shifted_left(u_t, right[:K], lane)
            along = [spread(0.5 * (a + b)) * (c - d) for a, b, c, d in zip(k_t, k_right, u_t, u_right)]
            entering = spread(0.5 * (left[K : K + 1] + k_t[0])) * (left[:K] - u_t[0])
            along_before = shifted_right(along, entering, lane)
            v_t = tiles(v_ref[pl.ds(i, 1), :])
            for t in range(nt):
                m = jnp.concatenate(
                    [u_t[t], flux[t] - flux_before[t], along[t] - along_before[t], spread(v_t[t]) * u_t[t]], 0
                )
                high = m.astype(BF16)
                low = (m - high.astype(F32)).astype(BF16)
                at = pl.ds(pl.multiple_of(step * wide + n * cols + 128 * t, 128), 128)
                mhl_ref[:C, at] = high
                mhl_ref[C:, at] = low
            u_now, k_now, flux_before = u_next, k_next, flux
        span = pl.ds(pl.multiple_of(step * wide, wide), wide)
        acc_ref[...] += lax.dot_general(
            mhl_ref[:C, span], mhl_ref[:, span], (((1,), (1,)), ((), ())), preferred_element_type=F32
        )

    cross = acc_ref[:, C:]
    total = (acc_ref[:, :C] + (cross + cross.T)) * scale
    lane32 = iota((32, C), 1)
    lane16 = iota((16, C), 1)
    gram_ref[:32, :] = total[:32]
    gram_ref[32:64, :] = jnp.where(lane32 >= 32, total[32:64], pltpu.roll(total[96:], 32, 1))
    gram_ref[64:, :] = jnp.where(lane16 >= 64, total[64:80], pltpu.roll(total[80:96], 64, 1))


def unpacked(packed):
    lane32 = iota((32, C), 1)
    lane16 = iota((16, C), 1)
    middle, tail = packed[32:64], packed[64:]
    upper = jnp.concatenate(
        [
            packed[:32],
            jnp.where(lane32 >= 32, middle, 0.0),
            jnp.where(lane16 >= 64, tail, 0.0),
            jnp.where(lane16 >= 64, pltpu.roll(tail, 64, 1), 0.0),
            jnp.where(lane32 >= 96, pltpu.roll(middle, 96, 1), 0.0),
        ],
        0,
    )
    return jnp.where(iota((C, C), 1) // 32 >= iota((C, C), 0) // 32, upper, upper.T)


def columns_and_gram(u_rows, conduct, potential, swapped, places, scale):
    rows, cols = conduct.shape
    near = pl.BlockSpec(memory_space=pltpu.VMEM)
    args = (u_rows, conduct, potential, *swapped)
    return pl.pallas_call(
        lambda *refs: gram_kernel(rows, cols, places, scale, *refs),
        name="gram",
        out_shape=[jax.ShapeDtypeStruct((80, C), F32), jax.ShapeDtypeStruct((2 * C, rows * cols), BF16)],
        in_specs=[near] * len(args),
        out_specs=[near] * 2,
        scratch_shapes=[pltpu.VMEM((C, 2 * C), F32)] + [pltpu.VMEM((K + 8, 128), F32)] * 2,
        compiler_params=pltpu.CompilerParams(vmem_limit_bytes=32 << 20),
    )(*args)


def factor(gram, after_panel):
    blocks = C // NB
    sub = iota((NB, C), 0)
    lane = iota((NB, C), 1)
    shape = (NB, C)
    a = [gram[NB * q : NB * q + NB] for q in range(blocks)]
    e = [jnp.where(lane == sub + NB * q, 1.0, 0.0).astype(F32) for q in range(blocks)]
    upper, inverse = [], []
    for p in range(blocks):
        col = lambda m, j: jnp.broadcast_to(m[:, NB * p + j : NB * p + j + 1], shape)
        row = lambda m, j: jnp.broadcast_to(m[j : j + 1, :], shape)
        cols = [col(a[p], j) for j in range(NB)]
        d = {(i, j): row(cols[j], i) for j in range(NB) for i in range(j + 1)}
        l, x = {}, {}
        for k in range(NB):
            r = lax.rsqrt(d[k, k])
            for j in range(k + 1, NB):
                l[k, j] = d[k, j] * r
            for i in range(k + 1, NB):
                for j in range(i, NB):
                    d[i, j] = d[i, j] - l[k, i] * l[k, j]
            x[k, k] = r
            for j in range(k):
                s = l[j, k] * x[j, j]
                for m in range(j + 1, k):
                    s = s + l[m, k] * x[m, j]
                x[k, j] = -(s * r)

        def combine(parts):
            out = []
            for k in range(NB):
                s = x[k, 0] * parts[0]
                for j in range(1, k + 1):
                    s = s + x[k, j] * parts[j]
                out.append(s)
            return out

        def solved(parts):
            out = []
            for j in range(NB):
                s = x[j, j] * parts[j]
                for k in range(j + 1, NB):
                    s = s + x[k, j] * parts[k]
                out.append(s)
            return out

        ra = combine([row(a[p], j) for j in range(NB)])
        re = combine([row(e[p], j) for j in range(NB)])
        ua, ue = ra[0], re[0]
        for k in range(1, NB):
            ua = jnp.where(sub == k, ra[k], ua)
            ue = jnp.where(sub == k, re[k], ue)
        upper.append(jnp.where(lane >= sub + NB * p, ua, 0.0))
        inverse.append(ue)
        wa, we = solved(ra), solved(re)
        for q in range(p + 1, blocks):
            c = [col(a[q], j) for j in range(NB)]
            sa, se = c[0] * wa[0], c[0] * we[0]
            for k in range(1, NB):
                sa, se = sa + c[k] * wa[k], se + c[k] * we[k]
            a[q], e[q] = a[q] - sa, e[q] - se
        after_panel(p, inverse)
    return upper, inverse


def finish_kernel(rows, cols, gram_ref, mhl_ref, out_ref, upper_ref, o_buf, xt_ref, xb_ref, out_sem):
    groups = rows // 8
    sides = cols // 128
    half = C // 2
    panels = C // NB

    def leave(g, t, part):
        place = out_ref.at[half * part : half * part + half, pl.ds(pl.multiple_of(8 * g, 8), 8), 128 * t : 128 * t + 128]
        source = o_buf.at[g, t, 8 * half * part : 8 * half * (part + 1)].reshape(half, 8, 128)
        return pltpu.make_async_copy(source, place, out_sem.at[g, t, part])

    def split(x):
        high = x.astype(BF16)
        low = (x - high.astype(F32)).astype(BF16)
        return jnp.concatenate([jnp.concatenate([high, high], 1), jnp.concatenate([low, jnp.zeros_like(low)], 1)], 0)

    def apply(g, part, left, depth):
        for n in range(8):
            at = pl.ds(pl.multiple_of((8 * g + n) * cols, cols), cols)
            high, low = mhl_ref[:depth, at], mhl_ref[C : C + depth, at]
            b = jnp.dot(left[...], jnp.concatenate([high, low], 0), preferred_element_type=F32)
            b = b[:half] + b[half:]
            for t in range(sides):
                o_buf[g, t, pl.ds(8 * half * part + n, half, stride=8), :] = b[:, 128 * t : 128 * t + 128]
        for t in range(sides):
            leave(g, t, part).start()

    top = []

    def after_panel(p, inverse):
        if p == panels // 2 - 1:
            xt_ref[...] = split(jnp.concatenate(inverse, 0)[:, :half])
        later = panels - panels // 2
        if p >= panels // 2:
            step = p - panels // 2
            for g in range(groups * step // later, groups * (step + 1) // later):
                apply(g, 0, xt_ref, half)

    upper, inverse = factor(unpacked(gram_ref[...]), after_panel)
    for p in range(panels):
        upper_ref[NB * p : NB * p + NB, :] = upper[p]
    xb_ref[...] = split(jnp.concatenate(inverse[panels // 2 :], 0))
    lax.fori_loop(0, groups, lambda g, c: (apply(g, 1, xb_ref, C), c)[1], 0, unroll=4)
    for g in range(groups):
        for t in range(sides):
            for part in range(2):
                leave(g, t, part).wait()


def finish(gram, mhl, rows, cols):
    near = pl.BlockSpec(memory_space=pltpu.VMEM)
    far = pl.BlockSpec(memory_space=pl.ANY)
    groups = rows // 8
    return pl.pallas_call(
        lambda *refs: finish_kernel(rows, cols, *refs),
        name="finish",
        out_shape=[jax.ShapeDtypeStruct((C, rows, cols), F32), jax.ShapeDtypeStruct((C, C), F32)],
        in_specs=[near, near],
        out_specs=[far, near],
        scratch_shapes=[
            pltpu.VMEM((groups, cols // 128, C * 8, 128), F32),
            pltpu.VMEM((C, C), BF16),
            pltpu.VMEM((C, 2 * C), BF16),
            pltpu.SemaphoreType.DMA((groups, cols // 128, 2)),
        ],
        compiler_params=pltpu.CompilerParams(vmem_limit_bytes=40 << 20),
    )(gram, mhl)


def exchanged(value, flips):
    across = lax.axis_size("gy")
    pairs = []
    for i in range(lax.axis_size("gx")):
        for j in range(across):
            along_x, along_y = flips[j % 2]
            pairs.append((i * across + j, (i ^ along_x) * across + (j ^ along_y)))
    return lax.ppermute(value, ("gx", "gy"), pairs)


def sum_over_devices(value):
    value = value + exchanged(value, ((0, 1), (0, 1)))
    along_x, along_y, along_z = ((1, 0), (2, 0), (3, 0)), ((0, 2), (0, 4), (0, 6)), ((4, 0), (8, 0), (12, 0))
    for group in (tuple(zip(along_x, along_y)), tuple(zip(along_y, along_x)), tuple(zip(along_z, along_z))):
        second = exchanged(value, group[1])
        first, third = exchanged(value, group[0]), exchanged(value, group[2])
        value = (value + first) + (second + third)
    return value + exchanged(value, ((28, 0), (28, 0)))


def on_device(mode_fields, conductance, potential):
    fields, rows, cols = mode_fields.shape
    along_x1, along_x2, along_y1, along_y2, u_rows, conduct, potent = edges(mode_fields, conductance, potential)
    places = {axis: lax.axis_size(axis) for axis in ("gx", "gy")}

    def swap(value, axis, first):
        n = places[axis]
        return lax.ppermute(value, axis, [(i, (i + 1 if (i % 2 == 0) == first else i - 1) % n) for i in range(n)])

    swapped = (
        swap(along_x1, "gx", True),
        swap(along_x2, "gx", False),
        swap(along_y1, "gy", True),
        swap(along_y2, "gy", False),
    )
    cells = rows * cols * places["gx"] * places["gy"]
    gram, mhl = columns_and_gram(u_rows, conduct, potent, swapped, places, 1.0 / cells)
    basis_field, scaled_factor = finish(sum_over_devices(gram), mhl, rows, cols)
    return (basis_field, scaled_factor)


def solution(mesh):
    placed = (P(None, "gx", "gy"), P("gx", "gy"), P("gx", "gy"))
    return jax.shard_map(
        on_device, mesh=mesh, in_specs=placed, out_specs=(P(None, "gx", "gy"), P()), check_vma=False
    )
```

```python
import jax
import jax.numpy as jnp
from jax import lax
from jax.experimental import pallas as pl
from jax.experimental.pallas import tpu as pltpu
from jax.sharding import PartitionSpec as P

F32 = jnp.float32
BF16 = jnp.bfloat16
K = 32
C = 128
NB = 8


def iota(shape, dim):
    return lax.broadcasted_iota(jnp.int32, shape, dim)


def edges_kernel(
    rows, cols, u_ref, k_ref, v_ref, x1_ref, x2_ref, y1_ref, y2_ref, rows_ref, ko_ref, vo_ref, buf, u_sem, c_sem
):
    sides = cols // 128
    groups = rows // 8

    def arrive(g, t):
        return pltpu.make_async_copy(
            u_ref.at[:, pl.ds(pl.multiple_of(8 * g, 8), 8), 128 * t : 128 * t + 128], buf.at[g, t].reshape(K, 8, 128), u_sem.at[g, t]
        )

    even_x = lax.axis_index("gx") % 2 == 0
    even_y = lax.axis_index("gy") % 2 == 0
    k_copy = pltpu.make_async_copy(k_ref, ko_ref, c_sem.at[0])
    v_copy = pltpu.make_async_copy(v_ref, vo_ref, c_sem.at[1])
    k_copy.start()
    for g in range(groups):
        for t in range(sides):
            arrive(g, t).start()
    v_copy.start()
    k_copy.wait()
    lane = iota((8, 128), 1)
    left = [jnp.zeros((8, 128), F32)] * (K // 8 + 1)
    right = [jnp.zeros((8, 128), F32)] * (K // 8 + 1)
    for i in range(rows):
        g, n = i // 8, i % 8
        if n == 0:
            for t in range(sides):
                arrive(g, t).wait()
        here, one_before = lane == i, lane == (i - 1) % 128
        parts = [buf[g, t, pl.ds(n, K, stride=8), :] for t in range(sides)]
        for t in range(sides):
            rows_ref[K * i : K * i + K, 128 * t : 128 * t + 128] = parts[t]
        conduct = jnp.broadcast_to(ko_ref[i : i + 1, :], (8, cols))
        if i == 0:
            top = jnp.concatenate([jnp.concatenate(parts, 1), conduct], 0)
        if i == rows - 1:
            bottom = jnp.concatenate([jnp.concatenate(parts, 1), conduct], 0)
        for b in range(K // 8 + 1):
            if b == K // 8:
                first, last = conduct[:, :128], conduct[:, cols - 128 :]
            else:
                first, last = parts[0][8 * b : 8 * b + 8], parts[-1][8 * b : 8 * b + 8]
            both = jnp.where(lane < 64, first, last)
            turned = pltpu.roll(both, i, 1) if i else both
            left[b] = jnp.where(here, turned, left[b])
            right[b] = jnp.where(one_before, turned, right[b])
    for b in range(K // 8 + 1):
        y1_ref[8 * b : 8 * b + 8, :] = jnp.where(even_y, right[b], left[b])
        y2_ref[8 * b : 8 * b + 8, :] = jnp.where(even_y, left[b], right[b])
    x1_ref[...] = jnp.where(even_x, bottom, top)
    x2_ref[...] = jnp.where(even_x, top, bottom)
    v_copy.wait()


def edges(fields, conduct, potential):
    rows, cols = conduct.shape
    far = pl.BlockSpec(memory_space=pltpu.HBM)
    near = pl.BlockSpec(memory_space=pltpu.VMEM)
    sizes = [(K + 8, cols)] * 2 + [(K + 8, 128)] * 2 + [(K * rows, cols)] + [(rows, cols)] * 2
    return pl.pallas_call(
        lambda *refs: edges_kernel(rows, cols, *refs),
        name="edges",
        out_shape=[jax.ShapeDtypeStruct(n, F32) for n in sizes],
        in_specs=[far] * 3,
        out_specs=[near] * 7,
        scratch_shapes=[
            pltpu.VMEM((rows // 8, cols // 128, K * 8, 128), F32),
            pltpu.SemaphoreType.DMA((rows // 8, cols // 128)),
            pltpu.SemaphoreType.DMA((2,)),
        ],
        compiler_params=pltpu.CompilerParams(vmem_limit_bytes=16 << 20),
    )(*[pltpu.with_memory_space_constraint(a, pltpu.HBM) for a in (fields, conduct, potential)])


def gram_kernel(
    rows, cols, places, scale, u_ref, k_ref, v_ref, x1_ref, x2_ref, y1_ref, y2_ref, gram_ref, mhl_ref, acc_ref, lf_ref, rt_ref
):
    per = 8
    wide = per * cols
    lane = iota((K, 128), 1)
    lane8 = iota((8, 128), 1)
    nt = cols // 128

    def field(i):
        return u_ref[pl.ds(pl.multiple_of(i * K, K), K), :]

    def tiles(a):
        return [a[:, 128 * t : 128 * t + 128] for t in range(nt)]

    def shifted_left(parts, edge, lanes):
        turned = [pltpu.roll(p, 127, 1) for p in parts] + [edge]
        return [jnp.where(lanes == 127, turned[t + 1], turned[t]) for t in range(nt)]

    def shifted_right(parts, edge, lanes):
        turned = [edge] + [pltpu.roll(p, 1, 1) for p in parts]
        return [jnp.where(lanes == 0, turned[t], turned[t + 1]) for t in range(nt)]

    def spread(row):
        return jnp.broadcast_to(row[0:1, :], (K, 128))

    def from_neighbours(axis, first, second):
        at, last = lax.axis_index(axis), places[axis] - 1
        even = at % 2 == 0
        before = jnp.where(at == 0, 0.0, jnp.where(even, second, first))
        return before, jnp.where(at == last, 0.0, jnp.where(even, first, second))

    up, down = from_neighbours("gx", x1_ref[...], x2_ref[...])
    lf_ref[...], rt_ref[...] = from_neighbours("gy", y1_ref[...], y2_ref[...])
    acc_ref[...] = jnp.zeros_like(acc_ref)

    @pl.loop(0, rows // per, unroll=True)
    def _(step):
        base = step * per
        is_first = step == 0
        is_last = step == rows // per - 1
        i_before = jnp.maximum(base - 1, 0)
        i_after = jnp.minimum(base + per, rows - 1)
        u_before = jnp.where(is_first, up[:K], field(i_before))
        k_before = jnp.where(is_first, up[K : K + 1], k_ref[pl.ds(i_before, 1), :])
        u_after = jnp.where(is_last, down[:K], field(i_after))
        k_after = jnp.where(is_last, down[K : K + 1], k_ref[pl.ds(i_after, 1), :])
        u_now = field(base)
        k_now = k_ref[pl.ds(base, 1), :]
        flux_before = [
            spread(a) * (b - c) for a, b, c in zip(tiles(0.5 * (k_before + k_now)), tiles(u_before), tiles(u_now))
        ]
        for n in range(per):
            i = base + n
            if n < per - 1:
                u_next, k_next = field(i + 1), k_ref[pl.ds(i + 1, 1), :]
            else:
                u_next, k_next = u_after, k_after
            u_t, k_t = tiles(u_now), tiles(k_now)
            flux = [spread(a) * (b - c) for a, b, c in zip(tiles(0.5 * (k_now + k_next)), u_t, tiles(u_next))]
            left = pltpu.roll(lf_ref[...], (129 - i) % 128, 1)
            right = pltpu.roll(rt_ref[...], 127 - i, 1)
            k_right = shifted_left(k_t, right[K : K + 1], lane8[:1])
            u_right = shifted_left(u_t, right[:K], lane)
            along = [spread(0.5 * (a + b)) * (c - d) for a, b, c, d in zip(k_t, k_right, u_t, u_right)]
            entering = spread(0.5 * (left[K : K + 1] + k_t[0])) * (left[:K] - u_t[0])
            along_before = shifted_right(along, entering, lane)
            v_t = tiles(v_ref[pl.ds(i, 1), :])
            for t in range(nt):
                m = jnp.concatenate(
                    [u_t[t], flux[t] - flux_before[t], along[t] - along_before[t], spread(v_t[t]) * u_t[t]], 0
                )
                high = m.astype(BF16)
                low = (m - high.astype(F32)).astype(BF16)
                at = pl.ds(pl.multiple_of(step * wide + n * cols + 128 * t, 128), 128)
                mhl_ref[:C, at] = high
                mhl_ref[C:, at] = low
            u_now, k_now, flux_before = u_next, k_next, flux
        span = pl.ds(pl.multiple_of(step * wide, wide), wide)
        acc_ref[...] += lax.dot_general(
            mhl_ref[:C, span], mhl_ref[:, span], (((1,), (1,)), ((), ())), preferred_element_type=F32
        )

    cross = acc_ref[:, C:]
    total = (acc_ref[:, :C] + (cross + cross.T)) * scale
    lane32 = iota((32, C), 1)
    lane16 = iota((16, C), 1)
    gram_ref[:32, :] = total[:32]
    gram_ref[32:64, :] = jnp.where(lane32 >= 32, total[32:64], pltpu.roll(total[96:], 32, 1))
    gram_ref[64:, :] = jnp.where(lane16 >= 64, total[64:80], pltpu.roll(total[80:96], 64, 1))


def unpacked(packed):
    lane32 = iota((32, C), 1)
    lane16 = iota((16, C), 1)
    middle, tail = packed[32:64], packed[64:]
    upper = jnp.concatenate(
        [
            packed[:32],
            jnp.where(lane32 >= 32, middle, 0.0),
            jnp.where(lane16 >= 64, tail, 0.0),
            jnp.where(lane16 >= 64, pltpu.roll(tail, 64, 1), 0.0),
            jnp.where(lane32 >= 96, pltpu.roll(middle, 96, 1), 0.0),
        ],
        0,
    )
    return jnp.where(iota((C, C), 1) // 32 >= iota((C, C), 0) // 32, upper, upper.T)


def columns_and_gram(u_rows, conduct, potential, swapped, places, scale):
    rows, cols = conduct.shape
    near = pl.BlockSpec(memory_space=pltpu.VMEM)
    args = (u_rows, conduct, potential, *swapped)
    return pl.pallas_call(
        lambda *refs: gram_kernel(rows, cols, places, scale, *refs),
        name="gram",
        out_shape=[jax.ShapeDtypeStruct((80, C), F32), jax.ShapeDtypeStruct((2 * C, rows * cols), BF16)],
        in_specs=[near] * len(args),
        out_specs=[near] * 2,
        scratch_shapes=[pltpu.VMEM((C, 2 * C), F32)] + [pltpu.VMEM((K + 8, 128), F32)] * 2,
        compiler_params=pltpu.CompilerParams(vmem_limit_bytes=32 << 20),
    )(*args)


def factor(gram, after_panel):
    blocks = C // NB
    sub = iota((NB, C), 0)
    lane = iota((NB, C), 1)
    shape = (NB, C)
    a = [gram[NB * q : NB * q + NB] for q in range(blocks)]
    e = [jnp.where(lane == sub + NB * q, 1.0, 0.0).astype(F32) for q in range(blocks)]
    upper, inverse = [], []

    def stacked(parts):
        out = parts[0]
        for k in range(1, NB):
            out = jnp.where(sub == k, parts[k], out)
        return out

    def three(value):
        first = value.astype(BF16).astype(F32)
        rest = value - first
        second = rest.astype(BF16).astype(F32)
        return first, second, rest - second

    for p in range(blocks):
        col = lambda m, j: jnp.broadcast_to(m[:, NB * p + j : NB * p + j + 1], shape)
        row = lambda m, j: jnp.broadcast_to(m[j : j + 1, :], shape)
        cols = [col(a[p], j) for j in range(NB)]
        d = {(i, j): row(cols[j], i) for j in range(NB) for i in range(j + 1)}
        l, x = {}, {}
        for k in range(NB):
            r = lax.rsqrt(d[k, k])
            for j in range(k + 1, NB):
                l[k, j] = d[k, j] * r
            for i in range(k + 1, NB):
                for j in range(i, NB):
                    d[i, j] = d[i, j] - l[k, i] * l[k, j]
            x[k, k] = r
            for j in range(k):
                s = l[j, k] * x[j, j]
                for m in range(j + 1, k):
                    s = s + l[m, k] * x[m, j]
                x[k, j] = -(s * r)

        def combine(parts):
            out = []
            for k in range(NB):
                s = x[k, 0] * parts[0]
                for j in range(1, k + 1):
                    s = s + x[k, j] * parts[j]
                out.append(s)
            return out

        def solved(parts):
            out = []
            for j in range(NB):
                s = x[j, j] * parts[j]
                for k in range(j + 1, NB):
                    s = s + x[k, j] * parts[k]
                out.append(s)
            return out

        ra = combine([row(a[p], j) for j in range(NB)])
        re = combine([row(e[p], j) for j in range(NB)])
        ua, ue = stacked(ra), stacked(re)
        upper.append(jnp.where(lane >= sub + NB * p, ua, 0.0))
        inverse.append(ue)
        wa, we = solved(ra), solved(re)
        near = min(p + 1 + 1, blocks)
        for q in range(p + 1, near):
            c = [col(a[q], j) for j in range(NB)]
            sa, se = c[0] * wa[0], c[0] * we[0]
            for k in range(1, NB):
                sa, se = sa + c[k] * wa[k], se + c[k] * we[k]
            a[q], e[q] = a[q] - sa, e[q] - se
        if near < blocks:
            w = jnp.concatenate([stacked(wa), stacked(we)], 1)
            p0, p1, p2 = three(a[p])
            w0, w1, w2 = three(w)
            delta = lax.dot_general(
                jnp.concatenate([p0, p0, p1, p1, p0, p2], 0).astype(BF16),
                jnp.concatenate([w0, w1, w0, w1, w2, w0], 0).astype(BF16),
                (((0,), (0,)), ((), ())),
                preferred_element_type=F32,
            )
            for q in range(near, blocks):
                a[q] = a[q] - delta[NB * q : NB * q + NB, :C]
                e[q] = e[q] - delta[NB * q : NB * q + NB, C:]
        after_panel(p, inverse)
    return upper, inverse


def finish_kernel(rows, cols, gram_ref, mhl_ref, out_ref, upper_ref, o_buf, xt_ref, xb_ref, out_sem):
    groups = rows // 8
    sides = cols // 128
    half = C // 2
    panels = C // NB

    def leave(g, t, part):
        place = out_ref.at[half * part : half * part + half, pl.ds(pl.multiple_of(8 * g, 8), 8), 128 * t : 128 * t + 128]
        source = o_buf.at[g, t, 8 * half * part : 8 * half * (part + 1)].reshape(half, 8, 128)
        return pltpu.make_async_copy(source, place, out_sem.at[g, t, part])

    def split(x):
        high = x.astype(BF16)
        low = (x - high.astype(F32)).astype(BF16)
        return jnp.concatenate([jnp.concatenate([high, high], 1), jnp.concatenate([low, jnp.zeros_like(low)], 1)], 0)

    def apply(g, part, left, depth):
        for n in range(8):
            at = pl.ds(pl.multiple_of((8 * g + n) * cols, cols), cols)
            high, low = mhl_ref[:depth, at], mhl_ref[C : C + depth, at]
            b = jnp.dot(left[...], jnp.concatenate([high, low], 0), preferred_element_type=F32)
            b = b[:half] + b[half:]
            for t in range(sides):
                o_buf[g, t, pl.ds(8 * half * part + n, half, stride=8), :] = b[:, 128 * t : 128 * t + 128]
        for t in range(sides):
            leave(g, t, part).start()

    top = []

    def after_panel(p, inverse):
        if p == panels // 2 - 1:
            xt_ref[...] = split(jnp.concatenate(inverse, 0)[:, :half])
        later = panels - panels // 2
        if p >= panels // 2:
            step = p - panels // 2
            for g in range(groups * step // later, groups * (step + 1) // later):
                apply(g, 0, xt_ref, half)

    upper, inverse = factor(unpacked(gram_ref[...]), after_panel)
    for p in range(panels):
        upper_ref[NB * p : NB * p + NB, :] = upper[p]
    xb_ref[...] = split(jnp.concatenate(inverse[panels // 2 :], 0))
    lax.fori_loop(0, groups, lambda g, c: (apply(g, 1, xb_ref, C), c)[1], 0, unroll=4)
    for g in range(groups):
        for t in range(sides):
            for part in range(2):
                leave(g, t, part).wait()


def finish(gram, mhl, rows, cols):
    near = pl.BlockSpec(memory_space=pltpu.VMEM)
    far = pl.BlockSpec(memory_space=pl.ANY)
    groups = rows // 8
    return pl.pallas_call(
        lambda *refs: finish_kernel(rows, cols, *refs),
        name="finish",
        out_shape=[jax.ShapeDtypeStruct((C, rows, cols), F32), jax.ShapeDtypeStruct((C, C), F32)],
        in_specs=[near, near],
        out_specs=[far, near],
        scratch_shapes=[
            pltpu.VMEM((groups, cols // 128, C * 8, 128), F32),
            pltpu.VMEM((C, C), BF16),
            pltpu.VMEM((C, 2 * C), BF16),
            pltpu.SemaphoreType.DMA((groups, cols // 128, 2)),
        ],
        compiler_params=pltpu.CompilerParams(vmem_limit_bytes=40 << 20),
    )(gram, mhl)


def exchanged(value, flips):
    across = lax.axis_size("gy")
    pairs = []
    for i in range(lax.axis_size("gx")):
        for j in range(across):
            along_x, along_y = flips[j % 2]
            pairs.append((i * across + j, (i ^ along_x) * across + (j ^ along_y)))
    return lax.ppermute(value, ("gx", "gy"), pairs)


def sum_over_devices(value):
    value = value + exchanged(value, ((0, 1), (0, 1)))
    along_x, along_y, along_z = ((1, 0), (2, 0), (3, 0)), ((0, 2), (0, 4), (0, 6)), ((4, 0), (8, 0), (12, 0))
    for group in (tuple(zip(along_x, along_y)), tuple(zip(along_y, along_x)), tuple(zip(along_z, along_z))):
        second = exchanged(value, group[1])
        first, third = exchanged(value, group[0]), exchanged(value, group[2])
        value = (value + first) + (second + third)
    return value + exchanged(value, ((28, 0), (28, 0)))


def on_device(mode_fields, conductance, potential):
    fields, rows, cols = mode_fields.shape
    along_x1, along_x2, along_y1, along_y2, u_rows, conduct, potent = edges(mode_fields, conductance, potential)
    places = {axis: lax.axis_size(axis) for axis in ("gx", "gy")}

    def swap(value, axis, first):
        n = places[axis]
        return lax.ppermute(value, axis, [(i, (i + 1 if (i % 2 == 0) == first else i - 1) % n) for i in range(n)])

    swapped = (
        swap(along_x1, "gx", True),
        swap(along_x2, "gx", False),
        swap(along_y1, "gy", True),
        swap(along_y2, "gy", False),
    )
    cells = rows * cols * places["gx"] * places["gy"]
    gram, mhl = columns_and_gram(u_rows, conduct, potent, swapped, places, 1.0 / cells)
    basis_field, scaled_factor = finish(sum_over_devices(gram), mhl, rows, cols)
    return (basis_field, scaled_factor)


def solution(mesh):
    placed = (P(None, "gx", "gy"), P("gx", "gy"), P("gx", "gy"))
    return jax.shard_map(
        on_device, mesh=mesh, in_specs=placed, out_specs=(P(None, "gx", "gy"), P()), check_vma=False
    )
```
